512 devices in a mesh: layer: 64 (over z, x), dp: 8 (over y, core).
Axes of the slice: x: 4, y: 4, z: 16, core: 2. Of those that a mesh axis runs over, the one named last changes fastest.
Arguments:
- states: float32 [64, 8, 24, 1536], P('layer', 'dp'), may hold values from -6 to 6
- adjoints: float32 [64, 8, 24, 1536], P('layer', 'dp'), may hold values from -6 to 6
- kernels: bfloat16 [256, 3, 3, 64, 64], P('layer'), may hold values from -0.25 to 0.25
- biases: float32 [256, 64], P('layer'), may hold values from -4 to 4
- coarse_gain: float32 [64, 64], P('layer'), may hold values from 0.01 to 1
Outputs:
- states_new: float32 [64, 8, 24, 1536], P('layer', 'dp')
- adjoints_new: float32 [64, 8, 24, 1536], P('layer', 'dp')
- kernel_grad: float32 [256, 3, 3, 64, 64], P('layer')
- bias_grad: float32 [256, 64], P('layer')
The draws below stay inside these ranges and needn't reach their ends.
All inputs are finite; a program needn't handle non-finite values.
Results may differ from the reference program's by a relative error of at most 0.0054.
Values sent between devices are 32-bit elements; how exact they have to be, the bound alone decides.
No kernel may reach another device: no remote copies, remote signals or barrier semaphores. Data moves between devices by JAX's collectives and lax.ppermute only.
A program may use at most 64 MiB of HBM per device.

```python
import jax
import jax.numpy as jnp
from jax import lax

CH = 64
HEIGHT = 24
WIDTH = 24
LPD = 4
NBLOCKS = 64
LAYERS = 256
IMAGES = 8


def draw_coarse_gain(key, part):
    subkeys = jax.random.split(key, 6)
    portion = 0.5
    lasting = jax.random.uniform(subkeys[0], (CH,)) < portion
    extent = jax.random.uniform(subkeys[1], (CH,), minval=0.2, maxval=1.0)
    spread = jnp.exp(jax.random.uniform(subkeys[2], (NBLOCKS, CH), minval=-0.7, maxval=0.7))
    slow_gain = jnp.exp(-extent[None, :] * spread / NBLOCKS)
    positions = jax.random.randint(subkeys[3], (2,), 0, NBLOCKS)
    struck = jnp.any(jnp.arange(NBLOCKS)[:, None] == positions[None, :], axis=1)
    factor = jax.random.uniform(subkeys[4], (NBLOCKS, CH), minval=0.6, maxval=0.8)
    slow_gain = jnp.where(struck[:, None], slow_gain * factor, slow_gain)
    fast_gain = jnp.exp(-jax.random.uniform(subkeys[5], (NBLOCKS, CH), minval=1.0, maxval=3.0))
    return jnp.where(lasting[None, :], slow_gain, fast_gain).astype(jnp.float32)


def block_levels(key, shape, cuts, smallest, largest):
    def one(axis_at, blocks):
        heights = jax.random.uniform(jax.random.fold_in(jax.random.fold_in(key, 6), axis_at), (blocks,), jnp.float32, smallest / len(cuts), largest / len(cuts))
        return jnp.repeat(jnp.exp(heights), shape[axis_at] // blocks).reshape((-1,) + (1,) * (len(shape) - axis_at - 1))

    loudness = one(*cuts[0])
    for cut in cuts[1:]:
        loudness = loudness * one(*cut)
    return loudness


def centred(key, shape, scale, most, shards=(), dtype=jnp.bfloat16):
    loudness = block_levels(key, shape, shards, -0.22, 0.18) if shards else 1.0
    values = jax.random.normal(key, shape, jnp.float32) * scale * loudness
    return jnp.minimum(jnp.maximum(values, -most), most).astype(dtype)


def setup_inputs(seed: int = 0) -> dict:
    key_of = jax.random.split(jax.random.key(seed), 6)
    return {
        "states": centred(key_of[0], (NBLOCKS, IMAGES, HEIGHT, WIDTH * CH), 1.0, 6.0, ((0, 64), (1, 8)), jnp.float32),
        "adjoints": centred(key_of[1], (NBLOCKS, IMAGES, HEIGHT, WIDTH * CH), 1.0, 6.0, ((0, 64), (1, 8)), jnp.float32),
        "kernels": centred(key_of[2], (LAYERS, 3, 3, CH, CH), (9 * CH) ** -0.5, 0.25, ((0, 64),)),
        "biases": centred(key_of[3], (LAYERS, CH), 1.0, 4.0, ((0, 64),), jnp.float32),
        "coarse_gain": draw_coarse_gain(jax.random.fold_in(key_of[5], 71), 0),
    }


step_size = 0.5


def correlate(field, kernel):
    return lax.conv_general_dilated(field, kernel, (1, 1), "SAME", dimension_numbers=("NHWC", "HWIO", "NHWC"), precision=lax.Precision.HIGHEST)


def rounded(values):
    return values.astype(jnp.bfloat16).astype(jnp.float32)


def activation(field, kernel, bias):
    return jnp.tanh(correlate(rounded(field), kernel.astype(jnp.float32)) + bias)


def kernel_terms(field, sens_round):
    rows_img = field.shape[1]
    cols_img = field.shape[2]
    channels = field.shape[3]
    padded = jnp.pad(rounded(field), ((0, 0), (1, 1), (1, 1), (0, 0)))
    patches = jnp.stack([padded[:, row:row + rows_img, col:col + cols_img] for row in range(3) for col in range(3)])
    summed = jnp.einsum("knhwi,nhwo->kio", patches, sens_round, precision=lax.Precision.HIGHEST)
    return summed.reshape(3, 3, channels, channels)


def block_pass(start, finish_adjoint, kernels, biases):
    field = start
    path = []
    acts = []
    depth_count = kernels.shape[0]
    for depth in range(depth_count):
        activ = activation(field, kernels[depth], biases[depth])
        path.append(field)
        acts.append(activ)
        field = field + step_size * activ
    adjoint = finish_adjoint
    kgrads = [None] * depth_count
    bgrads = [None] * depth_count
    for depth in reversed(range(depth_count)):
        sens = step_size * (1.0 - acts[depth] * acts[depth]) * adjoint
        sens_round = rounded(sens)
        flipped = kernels[depth][::-1, ::-1].transpose(0, 1, 3, 2).astype(jnp.float32)
        adjoint = adjoint + correlate(sens_round, flipped)
        kgrads[depth] = kernel_terms(path[depth], sens_round)
        bgrads[depth] = jnp.sum(sens, axis=(0, 1, 2))
    return field, adjoint, jnp.stack(kgrads), jnp.stack(bgrads)


def reference(states, adjoints, kernels, biases, coarse_gain):
    block_count, count_img, rows_img, flat = states.shape
    channels = kernels.shape[-1]
    cols_img = flat // channels
    shape_four = (count_img, rows_img, cols_img, channels)
    grouped_kernels = kernels.reshape(block_count, LPD, 3, 3, channels, channels)
    grouped_biases = biases.reshape(block_count, LPD, channels)

    def visit(carry, inputs):
        start, finish_adj, kern, bias = inputs
        finish, begin_adj, kgrad, bgrad = block_pass(start.reshape(shape_four), finish_adj.reshape(shape_four), kern, bias)
        return carry, (finish.reshape(count_img, rows_img, flat), begin_adj.reshape(count_img, rows_img, flat), kgrad, bgrad)

    _, (finish, begin_adj, kgrad, bgrad) = lax.scan(visit, jnp.zeros((), jnp.float32), (states, adjoints, grouped_kernels, grouped_biases))
    gain_rows = jnp.tile(coarse_gain, (1, cols_img)).reshape(block_count, 1, 1, flat)

    def forward_step(current, inputs):
        gain, older, finish_now = inputs
        following = gain * (current - older) + finish_now
        return following, following

    _, later = lax.scan(forward_step, states[0], (gain_rows[:-1], states[:-1], finish[:-1]))
    states_new = jnp.concatenate([states[:1], later], axis=0)

    def backward_step(current, inputs):
        gain, guess, begin_now = inputs
        earlier = gain * (current - guess) + begin_now
        return earlier, earlier

    _, before = lax.scan(backward_step, begin_adj[-1], (gain_rows[:-1], adjoints[:-1], begin_adj[:-1]), reverse=True)
    adjoints_new = jnp.concatenate([before, begin_adj[-1:]], axis=0)
    kernel_grad = kgrad.reshape(block_count * LPD, 3, 3, channels, channels) / count_img
    bias_grad = bgrad.reshape(block_count * LPD, channels) / count_img
    return states_new, adjoints_new, kernel_grad, bias_grad
```

```python
import functools

import jax
import jax.numpy as jnp
from jax import lax
from jax.experimental import pallas as pl
from jax.experimental.pallas import tpu as pltpu
from jax.sharding import PartitionSpec as P

STEP = 0.5
BF = jnp.bfloat16
F32 = jnp.float32
VMEM_BYTES = 12 * 1024 * 1024


def low_lanes(rows):
    return lax.broadcasted_iota(jnp.int32, (rows, 128), 1) < 64


def to_tiles(x):
    return jnp.concatenate([x[:, 128 * k : 128 * k + 128] for k in range(x.shape[1] // 128)], axis=0)


def patches(v, rows_img):
    count = v.shape[0]
    turned = pltpu.roll(v, 64, 1)
    edge = jnp.zeros((rows_img, 128), F32)
    mid = jnp.where(
        low_lanes(count + rows_img),
        jnp.concatenate([edge, turned], axis=0),
        jnp.concatenate([turned, edge], axis=0),
    )
    total = count + rows_img
    groups = total // rows_img
    where_y = lax.broadcasted_iota(jnp.int32, (groups, rows_img, 128), 1)
    up = pltpu.roll(mid, 1, 0).reshape(groups, rows_img, 128)
    up = jnp.where(where_y == 0, 0.0, up).reshape(total, 128)
    down = pltpu.roll(mid, total - 1, 0).reshape(groups, rows_img, 128)
    down = jnp.where(where_y == rows_img - 1, 0.0, down).reshape(total, 128)
    parts = []
    for t in (up, mid, down):
        parts.append(t[:count].astype(BF))
        parts.append(t[rows_img:].astype(BF))
    return jnp.concatenate(parts, axis=1)


def forward_weights(k_ref, layer):
    zero = jnp.zeros((64, 64), BF)
    rows = []
    for dy in range(3):
        tap = [k_ref[layer * 9 + dy * 3 + dx] for dx in range(3)]
        rows.append(jnp.concatenate([tap[0], zero], axis=1))
        rows.append(jnp.concatenate([tap[1], tap[0]], axis=1))
        rows.append(jnp.concatenate([tap[2], tap[1]], axis=1))
        rows.append(jnp.concatenate([zero, tap[2]], axis=1))
    return jnp.concatenate(rows, axis=0)


def backward_weights(k_ref, layer):
    zero = jnp.zeros((64, 64), BF)
    first, second = [], []
    for dy in range(3):
        tap = [k_ref[layer * 9 + (2 - dy) * 3 + dx] for dx in range(3)]
        first += [tap[2], tap[1], tap[0], zero]
        second += [zero, tap[2], tap[1], tap[0]]
    return jnp.concatenate(
        [jnp.concatenate(first, axis=1), jnp.concatenate(second, axis=1)], axis=0
    )


def pack(out_ref, value, gain):
    for r in range(4):
        out_ref[pl.ds(r, 64, stride=5), :] = value[64 * r : 64 * r + 64]
    low = low_lanes(32)
    rest = value[256:288]
    spread = jnp.broadcast_to(gain, (32, 128))
    extra = jnp.concatenate(
        [jnp.where(low, rest, spread), jnp.where(low, pltpu.roll(rest, 64, 1), spread)], axis=0
    )
    out_ref[pl.ds(4, 64, stride=5), :] = extra


def unpack(ref):
    extra = ref[pl.ds(4, 64, stride=5), :]
    rest = jnp.where(low_lanes(32), extra[:32], pltpu.roll(extra[32:], 64, 1))
    return jnp.concatenate([ref[pl.ds(r, 64, stride=5), :] for r in range(4)] + [rest], axis=0)


def from_tiles(out_ref, value, rows_img):
    for k in range(value.shape[0] // rows_img):
        out_ref[:, 128 * k : 128 * k + 128] = value[rows_img * k : rows_img * k + rows_img]


def doubled(row):
    return jnp.concatenate([row, row], axis=1)


def forward_kernel(depth_count, st_ref, k_ref, b_ref, g_ref, send_ref, act_ref, patch_ref):
    rows_img = st_ref.shape[0]
    start = to_tiles(st_ref[...])
    field = start
    bias = doubled(b_ref[...])
    for layer in range(depth_count):
        cells = patches(field, rows_img)
        patch_ref[layer] = cells
        total = jnp.dot(cells, forward_weights(k_ref, layer), preferred_element_type=F32)
        act = jnp.tanh(total + bias[layer : layer + 1])
        act_ref[layer] = act
        field = field + STEP * act
    gain = doubled(g_ref[...])
    gain = jnp.where(lax.axis_index("layer") == 0, jnp.zeros_like(gain), gain)
    pack(send_ref, field - gain * start, gain)


def backward_kernel(depth_count, blocks, adj_ref, act_ref, k_ref, g_ref, send_ref, sens_ref, bias_ref):
    rows_img = adj_ref.shape[0]
    start = to_tiles(adj_ref[...])
    adjoint = start
    sums = [None] * depth_count
    for layer in reversed(range(depth_count)):
        act = act_ref[layer]
        sens = STEP * (1.0 - act * act) * adjoint
        sens_ref[layer] = sens.astype(BF)
        total = jnp.sum(sens, axis=0, keepdims=True)
        sums[layer] = total + pltpu.roll(total, 64, 1)
        adjoint = adjoint + lax.dot_general(
            patches(sens, rows_img),
            backward_weights(k_ref, layer),
            (((1,), (1,)), ((), ())),
            preferred_element_type=F32,
        )
    gain = doubled(g_ref[...])
    gain = jnp.where(lax.axis_index("layer") == blocks - 1, jnp.zeros_like(gain), gain)
    pack(send_ref, adjoint - gain * start, gain)
    bias_ref[...] = jnp.concatenate(sums + [jnp.zeros((8 - depth_count, 128), F32)], axis=0)


CHUNK = 144
SPAN = 152


def gradient_kernel(depth_count, patch_ref, sens_ref, bias_ref, out_ref):
    low = low_lanes(192)
    for pair in range(depth_count // 2):
        both = [
            lax.dot_general(
                patch_ref[2 * pair + q],
                sens_ref[2 * pair + q],
                (((0,), (0,)), ((), ())),
                preferred_element_type=F32,
            )
            for q in range(2)
        ]
        for dy in range(3):
            one = both[0][256 * dy : 256 * dy + 256]
            two = both[1][256 * dy : 256 * dy + 256]
            tile = jnp.where(
                low,
                one[:192] + pltpu.roll(one[64:], 64, 1),
                pltpu.roll(two[:192], 64, 1) + two[64:],
            )
            at, done = pair * 576 + dy * 192, 0
            while done < 192:
                chunk, within = (at + done) // CHUNK, (at + done) % CHUNK
                size = min(CHUNK - within, 192 - done)
                out_ref[SPAN * chunk + within : SPAN * chunk + within + size] = tile[done : done + size]
                done += size
    for chunk in range(8):
        rows = slice(SPAN * chunk + CHUNK, SPAN * chunk + SPAN)
        out_ref[rows] = bias_ref[...] if chunk == 0 else jnp.zeros((SPAN - CHUNK, 128), F32)


def total_kernel(scale, in_ref, out_ref):
    total = in_ref[0]
    for other in range(1, in_ref.shape[0]):
        total = total + in_ref[other]
    total = total * scale
    for other in range(out_ref.shape[0]):
        out_ref[other] = total


def spread_kernel(depth_count, in_ref, grad_ref, bias_ref):
    bias_ref[...] = in_ref[CHUNK : CHUNK + depth_count, :64]
    for pair in range(depth_count // 2):
        for tap in range(9):
            at = pair * 576 + tap * 64
            pieces, done = [], 0
            while done < 64:
                chunk, within = (at + done) // CHUNK, (at + done) % CHUNK
                size = min(CHUNK - within, 64 - done)
                pieces.append(in_ref[SPAN * chunk + within : SPAN * chunk + within + size])
                done += size
            tile = pieces[0] if len(pieces) == 1 else jnp.concatenate(pieces, axis=0)
            grad_ref[18 * pair + tap] = tile[:, :64]
            grad_ref[18 * pair + 9 + tap] = pltpu.roll(tile, 64, 1)[:, :64]


def scan_kernel(blocks, reverse, in_ref, out_ref):
    extra = in_ref[pl.ds(4, blocks, stride=5), :]
    gains = jnp.where(low_lanes(blocks), pltpu.roll(extra, 64, 1), extra)
    value = jnp.zeros((5, 128), F32)
    for step in range(blocks):
        at = blocks - 1 - step if reverse else step
        rows = slice(5 * at, 5 * at + 5)
        following = gains[at : at + 1] * value + in_ref[rows]
        out_ref[rows] = following if reverse else value
        value = following


def finish_kernel(rows_img, in_ref, st_ref, out_ref):
    value = unpack(in_ref)
    from_tiles(out_ref, value, rows_img)

    @pl.when(lax.axis_index("layer") == 0)
    def _():
        out_ref[...] = st_ref[...]


def finish_last_kernel(rows_img, in_ref, out_ref):
    from_tiles(out_ref, unpack(in_ref), rows_img)


def call(kernel, name, outs, *args, flops=0):
    shapes = [jax.ShapeDtypeStruct(s, d) for s, d in outs]
    size = sum(a.size * a.dtype.itemsize for a in list(args) + shapes)
    return pl.pallas_call(
        kernel,
        out_shape=shapes,
        in_specs=[pl.BlockSpec(memory_space=pltpu.VMEM)] * len(args),
        out_specs=[pl.BlockSpec(memory_space=pltpu.VMEM)] * len(outs),
        compiler_params=pltpu.CompilerParams(vmem_limit_bytes=VMEM_BYTES),
        cost_estimate=pl.CostEstimate(flops=flops, bytes_accessed=size, transcendentals=0),
        name=name,
    )(*args)


def exchange(rows, axis, count):
    moved = lax.all_to_all(rows.reshape(count, -1), axis, 0, 0, tiled=True)
    return moved.reshape(rows.shape)


def body(states, adjoints, kernels, biases, coarse_gain):
    rows_img, flat = states.shape[2:]
    depth_count = kernels.shape[0]
    blocks, parts = lax.axis_size("layer"), lax.axis_size("dp")
    tiles = rows_img * flat // 128
    state = states.reshape(rows_img, flat)
    adjoint = adjoints.reshape(rows_img, flat)
    taps = kernels.reshape(depth_count * 9, 64, 64)
    field = ((tiles, 128), F32)
    packet = ((5 * blocks, 128), F32)
    image = ((rows_img, flat), F32)
    send, acts, cells = call(
        functools.partial(forward_kernel, depth_count),
        "forward",
        [packet, ((depth_count,) + field[0], F32), ((depth_count, tiles, 768), BF)],
        state, taps, biases, coarse_gain,
        flops=depth_count * tiles * 768 * 256,
    )
    came = exchange(send, "layer", blocks)
    send_adj, sens, bias = call(
        functools.partial(backward_kernel, depth_count, blocks),
        "backward",
        [packet, ((depth_count,) + field[0], BF), ((8, 128), F32)],
        adjoint, acts, taps, coarse_gain,
        flops=depth_count * tiles * 768 * 256,
    )
    came_adj = exchange(send_adj, "layer", blocks)
    (grads,) = call(
        functools.partial(gradient_kernel, depth_count),
        "gradient",
        [((SPAN * parts, 128), F32)],
        cells, sens, bias,
        flops=depth_count * tiles * 768 * 256,
    )
    shares = lax.all_to_all(grads.reshape(parts, SPAN, 128), "dp", 0, 0, tiled=True)
    (back,) = call(functools.partial(scan_kernel, blocks, False), "scan", [packet], came)
    home = exchange(back, "layer", blocks)
    (back_adj,) = call(functools.partial(scan_kernel, blocks, True), "scan_adj", [packet], came_adj)
    home_adj = exchange(back_adj, "layer", blocks)
    (sums,) = call(
        functools.partial(total_kernel, 1.0 / parts), "total", [((parts, SPAN, 128), F32)], shares
    )
    full = lax.all_to_all(sums, "dp", 0, 0, tiled=True)
    grad, bias_grad = call(
        functools.partial(spread_kernel, depth_count),
        "spread",
        [((depth_count * 9, 64, 64), F32), ((depth_count, 64), F32)],
        full.reshape(parts * SPAN, 128),
    )
    (states_new,) = call(functools.partial(finish_kernel, rows_img), "finish", [image], home, state)
    (adjoints_new,) = call(functools.partial(finish_last_kernel, rows_img), "finish_adj", [image], home_adj)
    return (
        states_new.reshape(states.shape),
        adjoints_new.reshape(adjoints.shape),
        grad.reshape(kernels.shape),
        bias_grad,
    )


def solution(mesh):
    return jax.shard_map(
        body,
        mesh=mesh,
        in_specs=(
            P("layer", "dp", None, None),
            P("layer", "dp", None, None),
            P("layer", None, None, None, None),
            P("layer", None),
            P("layer", None),
        ),
        out_specs=(
            P("layer", "dp", None, None),
            P("layer", "dp", None, None),
            P("layer", None, None, None, None),
            P("layer", None),
        ),
        check_vma=False,
    )
```

```python
import functools

import jax
import jax.numpy as jnp
from jax import lax
from jax.experimental import pallas as pl
from jax.experimental.pallas import tpu as pltpu
from jax.sharding import PartitionSpec as P

STEP = 0.5
BF = jnp.bfloat16
F32 = jnp.float32
VMEM_BYTES = 12 * 1024 * 1024
BLOCK_VMEM = 67_000_000


def low_lanes(rows):
    return lax.broadcasted_iota(jnp.int32, (rows, 128), 1) < 64


def to_tiles(x):
    return jnp.concatenate([x[:, 128 * k : 128 * k + 128] for k in range(x.shape[1] // 128)], axis=0)


def patches(v, rows_img):
    count = v.shape[0]
    turned = pltpu.roll(v, 64, 1)
    edge = jnp.zeros((rows_img, 128), F32)
    mid = jnp.where(
        low_lanes(count + rows_img),
        jnp.concatenate([edge, turned], axis=0),
        jnp.concatenate([turned, edge], axis=0),
    )
    total = count + rows_img
    groups = total // rows_img
    where_y = lax.broadcasted_iota(jnp.int32, (groups, rows_img, 128), 1)
    up = pltpu.roll(mid, 1, 0).reshape(groups, rows_img, 128)
    up = jnp.where(where_y == 0, 0.0, up).reshape(total, 128)
    down = pltpu.roll(mid, total - 1, 0).reshape(groups, rows_img, 128)
    down = jnp.where(where_y == rows_img - 1, 0.0, down).reshape(total, 128)
    parts = []
    for t in (up, mid, down):
        parts.append(t[:count].astype(BF))
        parts.append(t[rows_img:].astype(BF))
    return jnp.concatenate(parts, axis=1)


def forward_weights(k_ref, layer):
    zero = jnp.zeros((64, 64), BF)
    rows = []
    for dy in range(3):
        tap = [k_ref[layer * 9 + dy * 3 + dx] for dx in range(3)]
        rows.append(jnp.concatenate([tap[0], zero], axis=1))
        rows.append(jnp.concatenate([tap[1], tap[0]], axis=1))
        rows.append(jnp.concatenate([tap[2], tap[1]], axis=1))
        rows.append(jnp.concatenate([zero, tap[2]], axis=1))
    return jnp.concatenate(rows, axis=0)


def backward_weights(k_ref, layer):
    zero = jnp.zeros((64, 64), BF)
    first, second = [], []
    for dy in range(3):
        tap = [k_ref[layer * 9 + (2 - dy) * 3 + dx] for dx in range(3)]
        first += [tap[2], tap[1], tap[0], zero]
        second += [zero, tap[2], tap[1], tap[0]]
    return jnp.concatenate(
        [jnp.concatenate(first, axis=1), jnp.concatenate(second, axis=1)], axis=0
    )


def pack(out_ref, value, other, gain):
    for r in range(4):
        out_ref[pl.ds(r, 64, stride=10), :] = value[64 * r : 64 * r + 64]
        out_ref[pl.ds(5 + r, 64, stride=10), :] = other[64 * r : 64 * r + 64]
    low = low_lanes(32)
    rest, rest_other = value[256:288], other[256:288]
    out_ref[pl.ds(4, 64, stride=10), :] = jnp.concatenate(
        [
            jnp.where(low, rest, pltpu.roll(rest_other, 64, 1)),
            jnp.where(low, pltpu.roll(rest, 64, 1), rest_other),
        ],
        axis=0,
    )
    out_ref[pl.ds(9, 64, stride=10), :] = jnp.broadcast_to(gain, (64, 128))


def unpack(ref):
    low = low_lanes(32)
    extra = ref[pl.ds(4, 64, stride=9), :]
    rest = jnp.where(low, extra[:32], pltpu.roll(extra[32:], 64, 1))
    rest_other = jnp.where(low, pltpu.roll(extra[:32], 64, 1), extra[32:])
    value = [ref[pl.ds(r, 64, stride=9), :] for r in range(4)]
    other = [ref[pl.ds(5 + r, 64, stride=9), :] for r in range(4)]
    return jnp.concatenate(value + [rest], axis=0), jnp.concatenate(other + [rest_other], axis=0)


def from_tiles(out_ref, value, rows_img):
    for k in range(value.shape[0] // rows_img):
        out_ref[:, 128 * k : 128 * k + 128] = value[rows_img * k : rows_img * k + rows_img]


def doubled(row):
    return jnp.concatenate([row, row], axis=1)


def block_kernel(
    depth_count,
    blocks,
    st_hbm,
    adj_hbm,
    k_hbm,
    b_hbm,
    g_hbm,
    send_ref,
    patch_hbm,
    sens_hbm,
    bias_ref,
    st_ref,
    adj_ref,
    k_ref,
    b_ref,
    g_ref,
    act_ref,
    patch_ref,
    sens_ref,
    sems,
    patch_sems,
    sens_sems,
):
    pairs = [(k_hbm, k_ref), (st_hbm, st_ref), (b_hbm, b_ref), (adj_hbm, adj_ref), (g_hbm, g_ref)]
    copies = [pltpu.make_async_copy(a, b, sems.at[i]) for i, (a, b) in enumerate(pairs)]
    for copy in copies:
        copy.start()
    saves = []

    def save(ref, hbm, sem, layer):
        saves.append(pltpu.make_async_copy(ref.at[layer], hbm.at[layer], sem.at[layer]))
        saves[-1].start()

    rows_img = st_ref.shape[0]
    place = lax.axis_index("layer")
    for copy in copies[:3]:
        copy.wait()
    start = to_tiles(st_ref[...])
    field = start
    bias = doubled(b_ref[...])
    for layer in range(depth_count):
        cells = patches(field, rows_img)
        patch_ref[layer] = cells
        save(patch_ref, patch_hbm, patch_sems, layer)
        total = jnp.dot(cells, forward_weights(k_ref, layer), preferred_element_type=F32)
        act = jnp.tanh(total + bias[layer : layer + 1])
        act_ref[layer] = act
        field = field + STEP * act
    for copy in copies[3:]:
        copy.wait()
    gain = doubled(g_ref[...])
    lead = jnp.where(place == 0, jnp.zeros_like(gain), gain)
    tail = jnp.where(place == blocks - 1, jnp.zeros_like(gain), gain)
    offset = field - lead * start
    start_adj = to_tiles(adj_ref[...])
    adjoint = start_adj
    sums = [None] * depth_count
    for layer in reversed(range(depth_count)):
        act = act_ref[layer]
        sens = STEP * (1.0 - act * act) * adjoint
        sens_ref[layer] = sens.astype(BF)
        save(sens_ref, sens_hbm, sens_sems, layer)
        total = jnp.sum(sens, axis=0, keepdims=True)
        sums[layer] = total + pltpu.roll(total, 64, 1)
        adjoint = adjoint + lax.dot_general(
            patches(sens, rows_img),
            backward_weights(k_ref, layer),
            (((1,), (1,)), ((), ())),
            preferred_element_type=F32,
        )
    pack(send_ref, offset, adjoint - tail * start_adj, gain)
    bias_ref[...] = jnp.concatenate(sums + [jnp.zeros((8 - depth_count, 128), F32)], axis=0)
    for copy in saves:
        copy.wait()


def half_gradient(pair, patch_ref, sens_ref):
    low = low_lanes(192)
    both = [
        lax.dot_general(
            patch_ref[2 * pair + q],
            sens_ref[2 * pair + q],
            (((0,), (0,)), ((), ())),
            preferred_element_type=F32,
        )
        for q in range(2)
    ]
    tiles = []
    for dy in range(3):
        one = both[0][256 * dy : 256 * dy + 256]
        two = both[1][256 * dy : 256 * dy + 256]
        tiles.append(
            jnp.where(
                low,
                one[:192] + pltpu.roll(one[64:], 64, 1),
                pltpu.roll(two[:192], 64, 1) + two[64:],
            )
        )
    return tiles


def give_kernel(patch_ref, sens_ref, bias_ref, out_ref):
    core = lax.rem(lax.axis_index("dp"), 2)
    for dy, tile in enumerate(half_gradient(1 - core, patch_ref, sens_ref)):
        out_ref[192 * dy : 192 * dy + 192] = tile
    out_ref[576:584] = bias_ref[...]


def keep_kernel(patch_ref, sens_ref, bias_ref, got_ref, out_ref):
    core = lax.rem(lax.axis_index("dp"), 2)
    for dy, tile in enumerate(half_gradient(core, patch_ref, sens_ref)):
        rows = slice(192 * dy, 192 * dy + 192)
        out_ref[rows] = tile + got_ref[rows]
    out_ref[576:584] = bias_ref[...] + got_ref[576:584]


def total_kernel(scale, own_ref, one_ref, two_ref, three_ref, out_ref):
    out_ref[...] = ((own_ref[...] + two_ref[...]) + (one_ref[...] + three_ref[...])) * scale


def spread_kernel(depth_count, own_ref, other_ref, grad_ref, bias_ref):
    core = lax.rem(lax.axis_index("dp"), 2)
    bias_ref[...] = own_ref[576 : 576 + depth_count, :64]
    for pair, ref in ((core, own_ref), (1 - core, other_ref)):
        for tap in range(9):
            tile = ref[64 * tap : 64 * tap + 64]
            grad_ref[18 * pair + tap] = tile[:, :64]
            grad_ref[18 * pair + 9 + tap] = pltpu.roll(tile, 64, 1)[:, :64]


def scan_kernel(blocks, in_ref, out_ref, left_ref, right_ref):
    gains = in_ref[pl.ds(9, blocks, stride=10), :]
    value = jnp.zeros((5, 128), F32)
    other = jnp.zeros((5, 128), F32)
    for step in range(blocks):
        back = blocks - 1 - step
        out_ref[9 * step : 9 * step + 4] = value[:4]
        left_ref[step : step + 1] = value[4:]
        value = gains[step : step + 1] * value + in_ref[10 * step : 10 * step + 5]
        other = gains[back : back + 1] * other + in_ref[10 * back + 4 : 10 * back + 9]
        out_ref[9 * back + 5 : 9 * back + 9] = other[1:]
        right_ref[back : back + 1] = other[:1]
    out_ref[pl.ds(4, blocks, stride=9), :] = jnp.where(
        low_lanes(blocks), left_ref[...], right_ref[...]
    )


def finish_kernel(rows_img, in_ref, st_hbm, out_ref, adj_ref):
    value, other = unpack(in_ref)
    from_tiles(out_ref, value, rows_img)
    from_tiles(adj_ref, other, rows_img)

    @pl.when(lax.axis_index("layer") == 0)
    def _():
        pltpu.sync_copy(st_hbm, out_ref)


def call(kernel, outs, *args, flops=0, anywhere=(), away=(), scratch=(), room=VMEM_BYTES):
    shapes = [jax.ShapeDtypeStruct(s, d) for s, d in outs]
    size = sum(a.size * a.dtype.itemsize for a in list(args) + shapes)
    near = pl.BlockSpec(memory_space=pltpu.VMEM)
    far = pl.BlockSpec(memory_space=pltpu.HBM)
    return pl.pallas_call(
        kernel,
        out_shape=shapes,
        in_specs=[far if i in anywhere else near for i in range(len(args))],
        out_specs=[far if i in away else near for i in range(len(outs))],
        scratch_shapes=list(scratch),
        compiler_params=pltpu.CompilerParams(vmem_limit_bytes=room),
        cost_estimate=pl.CostEstimate(flops=flops, bytes_accessed=size, transcendentals=0),
    )(*args)


def exchange(rows, count):
    moved = lax.all_to_all(rows.reshape(count, -1), "layer", 0, 0, tiled=True)
    return moved.reshape(rows.shape)


def body(states, adjoints, kernels, biases, coarse_gain):
    rows_img, flat = states.shape[2:]
    depth_count = kernels.shape[0]
    blocks, parts = lax.axis_size("layer"), lax.axis_size("dp")
    tiles = rows_img * flat // 128
    state = states.reshape(rows_img, flat)
    adjoint = adjoints.reshape(rows_img, flat)
    taps = kernels.reshape(depth_count * 9, 64, 64)
    image = ((rows_img, flat), F32)
    half = ((584, 128), F32)
    work = tiles * 768 * 256
    swap = [(i, i ^ 1) for i in range(parts)]
    send, cells, sens, bias = call(
        functools.partial(block_kernel, depth_count, blocks),
        [
            ((10 * blocks, 128), F32),
            ((depth_count, tiles, 768), BF),
            ((depth_count, tiles, 128), BF),
            ((8, 128), F32),
        ],
        state, adjoint, taps, biases, coarse_gain,
        flops=2 * depth_count * work,
        anywhere=(0, 1, 2, 3, 4),
        away=(1, 2),
        room=BLOCK_VMEM,
        scratch=(
            pltpu.VMEM(image[0], F32),
            pltpu.VMEM(image[0], F32),
            pltpu.VMEM(taps.shape, BF),
            pltpu.VMEM(biases.shape, F32),
            pltpu.VMEM(coarse_gain.shape, F32),
            pltpu.VMEM((depth_count, tiles, 128), F32),
            pltpu.VMEM((depth_count, tiles, 768), BF),
            pltpu.VMEM((depth_count, tiles, 128), BF),
            pltpu.SemaphoreType.DMA((5,)),
            pltpu.SemaphoreType.DMA((depth_count,)),
            pltpu.SemaphoreType.DMA((depth_count,)),
        ),
    )
    came = exchange(send, blocks)
    (give,) = call(give_kernel, [half], cells, sens, bias, flops=2 * work)
    got = lax.ppermute(give, "dp", swap)
    (mine,) = call(keep_kernel, [half], cells, sens, bias, got, flops=2 * work)
    ring = []
    for hop in range(1, 4):
        path = [(i, (i + 2 * hop) % parts) for i in range(parts)]
        ring.append(lax.ppermute(mine, "dp", path))
    (back,) = call(
        functools.partial(scan_kernel, blocks),
        [((9 * blocks, 128), F32)],
        came,
        scratch=(pltpu.VMEM((blocks, 128), F32), pltpu.VMEM((blocks, 128), F32)),
    )
    home = exchange(back, blocks)
    (mine,) = call(functools.partial(total_kernel, 1.0 / parts), [half], mine, *ring)
    theirs = lax.ppermute(mine, "dp", swap)
    grad, bias_grad = call(
        functools.partial(spread_kernel, depth_count),
        [((depth_count * 9, 64, 64), F32), ((depth_count, 64), F32)],
        mine, theirs,
    )
    states_new, adjoints_new = call(
        functools.partial(finish_kernel, rows_img), [image, image], home, state,
        anywhere=(1,),
    )
    return (
        states_new.reshape(states.shape),
        adjoints_new.reshape(adjoints.shape),
        grad.reshape(kernels.shape),
        bias_grad,
    )


def solution(mesh):
    return jax.shard_map(
        body,
        mesh=mesh,
        in_specs=(
            P("layer", "dp", None, None),
            P("layer", "dp", None, None),
            P("layer", None, None, None, None),
            P("layer", None),
            P("layer", None),
        ),
        out_specs=(
            P("layer", "dp", None, None),
            P("layer", "dp", None, None),
            P("layer", None, None, None, None),
            P("layer", None),
        ),
        check_vma=False,
    )
```

```python
import functools

import jax
import jax.numpy as jnp
from jax import lax
from jax.experimental import pallas as pl
from jax.experimental.pallas import tpu as pltpu
from jax.sharding import PartitionSpec as P

STEP = 0.5
BF = jnp.bfloat16
F32 = jnp.float32
VMEM_BYTES = 12 * 1024 * 1024
BLOCK_VMEM = 67_000_000
ROW = 4
QUARTER = 72


def low_lanes(rows):
    return lax.broadcasted_iota(jnp.int32, (rows, 128), 1) < 64


def to_tiles(x):
    return jnp.concatenate([x[:, 128 * k : 128 * k + 128] for k in range(x.shape[1] // 128)], axis=0)


def patches(v, rows_img):
    count = v.shape[0]
    turned = pltpu.roll(v, 64, 1)
    edge = jnp.zeros((rows_img, 128), F32)
    mid = jnp.where(
        low_lanes(count + rows_img),
        jnp.concatenate([edge, turned], axis=0),
        jnp.concatenate([turned, edge], axis=0),
    )
    total = count + rows_img
    groups = total // rows_img
    where_y = lax.broadcasted_iota(jnp.int32, (groups, rows_img, 128), 1)
    up = pltpu.roll(mid, 1, 0).reshape(groups, rows_img, 128)
    up = jnp.where(where_y == 0, 0.0, up).reshape(total, 128)
    down = pltpu.roll(mid, total - 1, 0).reshape(groups, rows_img, 128)
    down = jnp.where(where_y == rows_img - 1, 0.0, down).reshape(total, 128)
    parts = []
    for t in (up, mid, down):
        parts.append(t[:count].astype(BF))
        parts.append(t[rows_img:].astype(BF))
    return jnp.concatenate(parts, axis=1)


def forward_weights(k_ref, layer):
    zero = jnp.zeros((64, 64), BF)
    rows = []
    for dy in range(3):
        tap = [k_ref[layer * 9 + dy * 3 + dx] for dx in range(3)]
        rows.append(jnp.concatenate([tap[0], zero], axis=1))
        rows.append(jnp.concatenate([tap[1], tap[0]], axis=1))
        rows.append(jnp.concatenate([tap[2], tap[1]], axis=1))
        rows.append(jnp.concatenate([zero, tap[2]], axis=1))
    return jnp.concatenate(rows, axis=0)


def backward_weights(k_ref, layer):
    zero = jnp.zeros((64, 64), BF)
    first, second = [], []
    for dy in range(3):
        tap = [k_ref[layer * 9 + (2 - dy) * 3 + dx] for dx in range(3)]
        first += [tap[2], tap[1], tap[0], zero]
        second += [zero, tap[2], tap[1], tap[0]]
    return jnp.concatenate(
        [jnp.concatenate(first, axis=1), jnp.concatenate(second, axis=1)], axis=0
    )


def pack(out_ref, count, value, other, gain):
    for r in range(4):
        out_ref[pl.ds(r, count, stride=10), :] = value[count * r : count * r + count]
        out_ref[pl.ds(5 + r, count, stride=10), :] = other[count * r : count * r + count]
    low = low_lanes(count // 2)
    rest, rest_other = value[4 * count :], other[4 * count :]
    out_ref[pl.ds(4, count, stride=10), :] = jnp.concatenate(
        [
            jnp.where(low, rest, pltpu.roll(rest_other, 64, 1)),
            jnp.where(low, pltpu.roll(rest, 64, 1), rest_other),
        ],
        axis=0,
    )
    out_ref[pl.ds(9, count, stride=10), :] = jnp.broadcast_to(gain, (count, 128))


def unpack(ref, count):
    low = low_lanes(count // 2)
    extra = ref[pl.ds(4, count, stride=9), :]
    top, bottom = extra[: count // 2], extra[count // 2 :]
    rest = jnp.where(low, top, pltpu.roll(bottom, 64, 1))
    rest_other = jnp.where(low, pltpu.roll(top, 64, 1), bottom)
    value = [ref[pl.ds(r, count, stride=9), :] for r in range(4)]
    other = [ref[pl.ds(5 + r, count, stride=9), :] for r in range(4)]
    return jnp.concatenate(value + [rest], axis=0), jnp.concatenate(other + [rest_other], axis=0)


def from_tiles(out_ref, value, rows_img):
    for k in range(value.shape[0] // rows_img):
        out_ref[:, 128 * k : 128 * k + 128] = value[rows_img * k : rows_img * k + rows_img]


def doubled(row):
    return jnp.concatenate([row, row], axis=1)


def half_gradient(out_ref, cells, senses, bias_rows):
    low = low_lanes(192)
    one, two = [
        lax.dot_general(c, s, (((0,), (0,)), ((), ())), preferred_element_type=F32)
        for c, s in zip(cells, senses)
    ]
    for dy in range(3):
        first = one[256 * dy : 256 * dy + 256]
        second = two[256 * dy : 256 * dy + 256]
        out_ref[192 * dy : 192 * dy + 192] = jnp.where(
            low,
            first[:192] + pltpu.roll(first[64:], 64, 1),
            pltpu.roll(second[:192], 64, 1) + second[64:],
        )
    out_ref[576:584] = bias_rows


def block_kernel(
    depth_count,
    blocks,
    st_hbm,
    adj_hbm,
    k_hbm,
    b_hbm,
    g_hbm,
    send_ref,
    give_ref,
    keep_ref,
    st_ref,
    adj_ref,
    k_ref,
    b_ref,
    g_ref,
    act_ref,
    patch_ref,
    sens_ref,
    sems,
):
    pairs = [(k_hbm, k_ref), (st_hbm, st_ref), (b_hbm, b_ref), (adj_hbm, adj_ref), (g_hbm, g_ref)]
    copies = [pltpu.make_async_copy(a, b, sems.at[i]) for i, (a, b) in enumerate(pairs)]
    for copy in copies:
        copy.start()
    rows_img = st_ref.shape[0]
    place = lax.axis_index("layer")
    core = lax.rem(lax.axis_index("dp"), 2)
    for copy in copies[:3]:
        copy.wait()
    start = to_tiles(st_ref[...])
    field = start
    bias = doubled(b_ref[...])
    for layer in range(depth_count):
        cells = patches(field, rows_img)
        patch_ref[layer] = cells
        total = jnp.dot(cells, forward_weights(k_ref, layer), preferred_element_type=F32)
        act = jnp.tanh(total + bias[layer : layer + 1])
        act_ref[layer] = act
        field = field + STEP * act
    for copy in copies[3:]:
        copy.wait()
    gain = doubled(g_ref[...])
    lead = jnp.where(place == 0, jnp.zeros_like(gain), gain)
    tail = jnp.where(place == blocks - 1, jnp.zeros_like(gain), gain)
    offset = field - lead * start
    start_adj = to_tiles(adj_ref[...])
    adjoint = start_adj
    sums = [None] * depth_count
    for layer in reversed(range(depth_count)):
        act = act_ref[layer]
        sens = STEP * (1.0 - act * act) * adjoint
        sens_ref[layer] = sens.astype(BF)
        total = jnp.sum(sens, axis=0, keepdims=True)
        sums[layer] = total + pltpu.roll(total, 64, 1)
        adjoint = adjoint + lax.dot_general(
            patches(sens, rows_img),
            backward_weights(k_ref, layer),
            (((1,), (1,)), ((), ())),
            preferred_element_type=F32,
        )
    back = adjoint - tail * start_adj
    for part in range(ROW):
        rows = slice(QUARTER * part, QUARTER * part + QUARTER)
        send_ref[part, :QUARTER] = offset[rows]
        send_ref[part, QUARTER : 2 * QUARTER] = back[rows]
        send_ref[part, 2 * QUARTER :] = jnp.broadcast_to(gain, (8, 128))
    bias_rows = jnp.concatenate(sums + [jnp.zeros((8 - depth_count, 128), F32)], axis=0)
    for pair, ref in ((1 - core, give_ref), (core, keep_ref)):
        half_gradient(
            ref,
            [patch_ref[2 * pair + q] for q in range(2)],
            [sens_ref[2 * pair + q] for q in range(2)],
            bias_rows,
        )


def keep_kernel(keep_ref, got_ref, out_ref):
    out_ref[...] = keep_ref[...] + got_ref[...]


def total_kernel(scale, own_ref, one_ref, two_ref, three_ref, out_ref):
    out_ref[...] = ((own_ref[...] + two_ref[...]) + (one_ref[...] + three_ref[...])) * scale


def spread_kernel(depth_count, own_ref, other_ref, grad_ref, bias_ref):
    core = lax.rem(lax.axis_index("dp"), 2)
    bias_ref[...] = own_ref[576 : 576 + depth_count, :64]
    for pair, ref in ((core, own_ref), (1 - core, other_ref)):
        for tap in range(9):
            tile = ref[64 * tap : 64 * tap + 64]
            grad_ref[18 * pair + tap] = tile[:, :64]
            grad_ref[18 * pair + 9 + tap] = pltpu.roll(tile, 64, 1)[:, :64]


def row_parts(ref, part):
    return (
        ref[part, :QUARTER],
        ref[part, QUARTER : 2 * QUARTER],
        ref[part, 2 * QUARTER : 2 * QUARTER + 1],
    )


def compose_kernel(count, in_ref, out_ref):
    parts = [row_parts(in_ref, part) for part in range(ROW)]
    value, other, gain = parts[0][0], parts[-1][1], parts[0][2]
    for ahead, _, factor in parts[1:]:
        value = factor * value + ahead
        gain = gain * factor
    for _, behind, factor in reversed(parts[:-1]):
        other = factor * other + behind
    pack(out_ref, count, value, other, gain)


def scan_kernel(count, in_ref, out_ref, left_ref, right_ref):
    gains = in_ref[pl.ds(9, count, stride=10), :]
    value = jnp.zeros((5, 128), F32)
    other = jnp.zeros((5, 128), F32)
    for step in range(count):
        back = count - 1 - step
        out_ref[9 * step : 9 * step + 4] = value[:4]
        left_ref[step : step + 1] = value[4:]
        out_ref[9 * back + 5 : 9 * back + 9] = other[1:]
        right_ref[back : back + 1] = other[:1]
        value = gains[step : step + 1] * value + in_ref[10 * step : 10 * step + 5]
        other = gains[back : back + 1] * other + in_ref[10 * back + 4 : 10 * back + 9]
    out_ref[pl.ds(4, count, stride=9), :] = jnp.where(
        low_lanes(count), left_ref[...], right_ref[...]
    )


def expand_kernel(count, home_ref, came_ref, out_ref):
    value, other = unpack(home_ref, count)
    for part in range(ROW):
        back = ROW - 1 - part
        ahead, _, gain = row_parts(came_ref, part)
        out_ref[part, :QUARTER] = value
        value = gain * value + ahead
        _, behind, gain = row_parts(came_ref, back)
        other = gain * other + behind
        out_ref[back, QUARTER:] = other


def finish_kernel(rows_img, in_ref, st_hbm, out_ref, adj_ref):
    value = jnp.concatenate([in_ref[part, :QUARTER] for part in range(ROW)], axis=0)
    other = jnp.concatenate([in_ref[part, QUARTER:] for part in range(ROW)], axis=0)
    from_tiles(out_ref, value, rows_img)
    from_tiles(adj_ref, other, rows_img)

    @pl.when(lax.axis_index("layer") == 0)
    def _():
        pltpu.sync_copy(st_hbm, out_ref)


def call(kernel, outs, *args, flops=0, anywhere=(), away=(), scratch=(), room=VMEM_BYTES):
    shapes = [jax.ShapeDtypeStruct(s, d) for s, d in outs]
    size = sum(a.size * a.dtype.itemsize for a in list(args) + shapes)
    near = pl.BlockSpec(memory_space=pltpu.VMEM)
    far = pl.BlockSpec(memory_space=pltpu.HBM)
    return pl.pallas_call(
        kernel,
        out_shape=shapes,
        in_specs=[far if i in anywhere else near for i in range(len(args))],
        out_specs=[far if i in away else near for i in range(len(outs))],
        scratch_shapes=list(scratch),
        compiler_params=pltpu.CompilerParams(vmem_limit_bytes=room),
        cost_estimate=pl.CostEstimate(flops=flops, bytes_accessed=size, transcendentals=0),
    )(*args)


def exchange(array, groups):
    count = len(groups[0])
    moved = lax.all_to_all(
        array.reshape(count, -1, 128) if array.ndim == 3 else array.reshape(count, -1),
        "layer",
        0,
        0,
        axis_index_groups=groups,
        tiled=True,
    )
    return moved.reshape(array.shape)


def body(states, adjoints, kernels, biases, coarse_gain):
    rows_img, flat = states.shape[2:]
    depth_count = kernels.shape[0]
    blocks, parts = lax.axis_size("layer"), lax.axis_size("dp")
    tiles = rows_img * flat // 128
    count = blocks // ROW
    rows = [[z * ROW + x for x in range(ROW)] for z in range(count)]
    columns = [[z * ROW + x for z in range(count)] for x in range(ROW)]
    state = states.reshape(rows_img, flat)
    adjoint = adjoints.reshape(rows_img, flat)
    taps = kernels.reshape(depth_count * 9, 64, 64)
    image = ((rows_img, flat), F32)
    half = ((584, 128), F32)
    swap = [(i, i ^ 1) for i in range(parts)]
    send, give, keep = call(
        functools.partial(block_kernel, depth_count, blocks),
        [((ROW, 2 * QUARTER + 8, 128), F32), half, half],
        state, adjoint, taps, biases, coarse_gain,
        flops=3 * depth_count * tiles * 768 * 256,
        anywhere=(0, 1, 2, 3, 4),
        room=BLOCK_VMEM,
        scratch=(
            pltpu.VMEM(image[0], F32),
            pltpu.VMEM(image[0], F32),
            pltpu.VMEM(taps.shape, BF),
            pltpu.VMEM(biases.shape, F32),
            pltpu.VMEM(coarse_gain.shape, F32),
            pltpu.VMEM((depth_count, tiles, 128), F32),
            pltpu.VMEM((depth_count, tiles, 768), BF),
            pltpu.VMEM((depth_count, tiles, 128), BF),
            pltpu.SemaphoreType.DMA((5,)),
        ),
    )
    came = exchange(send, rows)
    got = lax.ppermute(give, "dp", swap)
    (mine,) = call(keep_kernel, [half], keep, got)
    (totals,) = call(functools.partial(compose_kernel, count), [((10 * count, 128), F32)], came)
    column = exchange(totals, columns)
    ring = []
    for hop in range(1, 4):
        path = [(i, (i + 2 * hop) % parts) for i in range(parts)]
        ring.append(lax.ppermute(mine, "dp", path))
    (before,) = call(
        functools.partial(scan_kernel, count),
        [((9 * count, 128), F32)],
        column,
        scratch=(pltpu.VMEM((count, 128), F32), pltpu.VMEM((count, 128), F32)),
    )
    home = exchange(before, columns)
    (mine,) = call(functools.partial(total_kernel, 1.0 / parts), [half], mine, *ring)
    theirs = lax.ppermute(mine, "dp", swap)
    (spread,) = call(
        functools.partial(expand_kernel, count),
        [((ROW, 2 * QUARTER, 128), F32)],
        home, came,
    )
    result = exchange(spread, rows)
    grad, bias_grad = call(
        functools.partial(spread_kernel, depth_count),
        [((depth_count * 9, 64, 64), F32), ((depth_count, 64), F32)],
        mine, theirs,
    )
    states_new, adjoints_new = call(
        functools.partial(finish_kernel, rows_img), [image, image], result, state,
        anywhere=(1,),
    )
    return (
        states_new.reshape(states.shape),
        adjoints_new.reshape(adjoints.shape),
        grad.reshape(kernels.shape),
        bias_grad,
    )


def solution(mesh):
    return jax.shard_map(
        body,
        mesh=mesh,
        in_specs=(
            P("layer", "dp", None, None),
            P("layer", "dp", None, None),
            P("layer", None, None, None, None),
            P("layer", None),
            P("layer", None),
        ),
        out_specs=(
            P("layer", "dp", None, None),
            P("layer", "dp", None, None),
            P("layer", None, None, None, None),
            P("layer", None),
        ),
        check_vma=False,
    )
```

```python
import functools

import jax
import jax.numpy as jnp
from jax import lax
from jax.experimental import pallas as pl
from jax.experimental.pallas import tpu as pltpu
from jax.sharding import PartitionSpec as P

STEP = 0.5
BF = jnp.bfloat16
F32 = jnp.float32
VMEM_BYTES = 12 * 1024 * 1024
BLOCK_VMEM = 67_000_000
ROW = 4
QUARTER = 72


def low_lanes(rows):
    return lax.broadcasted_iota(jnp.int32, (rows, 128), 1) < 64


def to_tiles(x):
    return jnp.concatenate([x[:, 128 * k : 128 * k + 128] for k in range(x.shape[1] // 128)], axis=0)


def patches(v, rows_img):
    count = v.shape[0]
    turned = pltpu.roll(v, 64, 1)
    edge = jnp.zeros((rows_img, 128), F32)
    mid = jnp.where(
        low_lanes(count + rows_img),
        jnp.concatenate([edge, turned], axis=0),
        jnp.concatenate([turned, edge], axis=0),
    )
    total = count + rows_img
    groups = total // rows_img
    where_y = lax.broadcasted_iota(jnp.int32, (groups, rows_img, 128), 1)
    up = pltpu.roll(mid, 1, 0).reshape(groups, rows_img, 128)
    up = jnp.where(where_y == 0, 0.0, up).reshape(total, 128)
    down = pltpu.roll(mid, total - 1, 0).reshape(groups, rows_img, 128)
    down = jnp.where(where_y == rows_img - 1, 0.0, down).reshape(total, 128)
    parts = []
    for t in (up, mid, down):
        parts.append(t[:count].astype(BF))
        parts.append(t[rows_img:].astype(BF))
    return jnp.concatenate(parts, axis=1)


def forward_weights(k_ref, layer):
    zero = jnp.zeros((64, 64), BF)
    rows = []
    for dy in range(3):
        tap = [k_ref[layer * 9 + dy * 3 + dx] for dx in range(3)]
        rows.append(jnp.concatenate([tap[0], zero], axis=1))
        rows.append(jnp.concatenate([tap[1], tap[0]], axis=1))
        rows.append(jnp.concatenate([tap[2], tap[1]], axis=1))
        rows.append(jnp.concatenate([zero, tap[2]], axis=1))
    return jnp.concatenate(rows, axis=0)


def backward_weights(k_ref, layer):
    zero = jnp.zeros((64, 64), BF)
    first, second = [], []
    for dy in range(3):
        tap = [k_ref[layer * 9 + (2 - dy) * 3 + dx] for dx in range(3)]
        first += [tap[2], tap[1], tap[0], zero]
        second += [zero, tap[2], tap[1], tap[0]]
    return jnp.concatenate(
        [jnp.concatenate(first, axis=1), jnp.concatenate(second, axis=1)], axis=0
    )


def pack(out_ref, count, value, other, gain):
    for r in range(4):
        out_ref[pl.ds(r, count, stride=10), :] = value[count * r : count * r + count]
        out_ref[pl.ds(5 + r, count, stride=10), :] = other[count * r : count * r + count]
    low = low_lanes(count // 2)
    rest, rest_other = value[4 * count :], other[4 * count :]
    out_ref[pl.ds(4, count, stride=10), :] = jnp.concatenate(
        [
            jnp.where(low, rest, pltpu.roll(rest_other, 64, 1)),
            jnp.where(low, pltpu.roll(rest, 64, 1), rest_other),
        ],
        axis=0,
    )
    out_ref[pl.ds(9, count, stride=10), :] = jnp.broadcast_to(gain, (count, 128))


def unpack(ref, count):
    low = low_lanes(count // 2)
    extra = ref[pl.ds(4, count, stride=9), :]
    top, bottom = extra[: count // 2], extra[count // 2 :]
    rest = jnp.where(low, top, pltpu.roll(bottom, 64, 1))
    rest_other = jnp.where(low, pltpu.roll(top, 64, 1), bottom)
    value = [ref[pl.ds(r, count, stride=9), :] for r in range(4)]
    other = [ref[pl.ds(5 + r, count, stride=9), :] for r in range(4)]
    return jnp.concatenate(value + [rest], axis=0), jnp.concatenate(other + [rest_other], axis=0)


def from_tiles(out_ref, value, rows_img):
    for k in range(value.shape[0] // rows_img):
        out_ref[:, 128 * k : 128 * k + 128] = value[rows_img * k : rows_img * k + rows_img]


def doubled(row):
    return jnp.concatenate([row, row], axis=1)


def half_gradient(out_ref, cells, senses, bias_rows):
    low = low_lanes(192)
    one, two = [
        lax.dot_general(c, s, (((0,), (0,)), ((), ())), preferred_element_type=F32)
        for c, s in zip(cells, senses)
    ]
    for dy in range(3):
        first = one[256 * dy : 256 * dy + 256]
        second = two[256 * dy : 256 * dy + 256]
        out_ref[192 * dy : 192 * dy + 192] = jnp.where(
            low,
            first[:192] + pltpu.roll(first[64:], 64, 1),
            pltpu.roll(second[:192], 64, 1) + second[64:],
        )
    out_ref[576:584] = bias_rows


def block_kernel(
    depth_count,
    blocks,
    st_hbm,
    adj_hbm,
    k_hbm,
    b_hbm,
    g_hbm,
    send_ref,
    give_ref,
    keep_ref,
    st_ref,
    adj_ref,
    k_ref,
    b_ref,
    g_ref,
    act_ref,
    patch_ref,
    sens_ref,
    sems,
):
    pairs = [(k_hbm, k_ref), (st_hbm, st_ref), (b_hbm, b_ref), (adj_hbm, adj_ref), (g_hbm, g_ref)]
    copies = [pltpu.make_async_copy(a, b, sems.at[i]) for i, (a, b) in enumerate(pairs)]
    for copy in copies:
        copy.start()
    rows_img = st_ref.shape[0]
    place = lax.axis_index("layer")
    core = lax.rem(lax.axis_index("dp"), 2)
    for copy in copies[:3]:
        copy.wait()
    start = to_tiles(st_ref[...])
    field = start
    bias = doubled(b_ref[...])
    for layer in range(depth_count):
        cells = patches(field, rows_img)
        patch_ref[layer] = cells
        total = jnp.dot(cells, forward_weights(k_ref, layer), preferred_element_type=F32)
        act = jnp.tanh(total + bias[layer : layer + 1])
        act_ref[layer] = act
        field = field + STEP * act
    for copy in copies[3:]:
        copy.wait()
    gain = doubled(g_ref[...])
    lead = jnp.where(place == 0, jnp.zeros_like(gain), gain)
    tail = jnp.where(place == blocks - 1, jnp.zeros_like(gain), gain)
    offset = field - lead * start
    start_adj = to_tiles(adj_ref[...])
    adjoint = start_adj
    sums = [None] * depth_count
    for layer in reversed(range(depth_count)):
        act = act_ref[layer]
        sens = STEP * (1.0 - act * act) * adjoint
        sens_ref[layer] = sens.astype(BF)
        total = jnp.sum(sens, axis=0, keepdims=True)
        sums[layer] = total + pltpu.roll(total, 64, 1)
        adjoint = adjoint + lax.dot_general(
            patches(sens, rows_img),
            backward_weights(k_ref, layer),
            (((1,), (1,)), ((), ())),
            preferred_element_type=F32,
        )
    back = adjoint - tail * start_adj
    for part in range(ROW):
        rows = slice(QUARTER * part, QUARTER * part + QUARTER)
        send_ref[part, :QUARTER] = offset[rows]
        send_ref[part, QUARTER : 2 * QUARTER] = back[rows]
        send_ref[part, 2 * QUARTER :] = jnp.broadcast_to(gain, (8, 128))
    bias_rows = jnp.concatenate(sums + [jnp.zeros((8 - depth_count, 128), F32)], axis=0)
    for pair, ref in ((1 - core, give_ref), (core, keep_ref)):
        half_gradient(
            ref,
            [patch_ref[2 * pair + q] for q in range(2)],
            [sens_ref[2 * pair + q] for q in range(2)],
            bias_rows,
        )


def add_kernel(scale, own_ref, other_ref, out_ref):
    out_ref[...] = (own_ref[...] + other_ref[...]) * scale


def spread_kernel(depth_count, own_ref, other_ref, grad_ref, bias_ref):
    core = lax.rem(lax.axis_index("dp"), 2)
    bias_ref[...] = own_ref[576 : 576 + depth_count, :64]
    for pair, ref in ((core, own_ref), (1 - core, other_ref)):
        for tap in range(9):
            tile = ref[64 * tap : 64 * tap + 64]
            grad_ref[18 * pair + tap] = tile[:, :64]
            grad_ref[18 * pair + 9 + tap] = pltpu.roll(tile, 64, 1)[:, :64]


def row_parts(ref, part):
    return (
        ref[part, :QUARTER],
        ref[part, QUARTER : 2 * QUARTER],
        ref[part, 2 * QUARTER : 2 * QUARTER + 1],
    )


def compose_kernel(count, in_ref, out_ref):
    parts = [row_parts(in_ref, part) for part in range(ROW)]
    value, other, gain = parts[0][0], parts[-1][1], parts[0][2]
    for ahead, _, factor in parts[1:]:
        value = factor * value + ahead
        gain = gain * factor
    for _, behind, factor in reversed(parts[:-1]):
        other = factor * other + behind
    pack(out_ref, count, value, other, gain)


def scan_kernel(count, in_ref, out_ref, left_ref, right_ref):
    gains = in_ref[pl.ds(9, count, stride=10), :]
    value = jnp.zeros((5, 128), F32)
    other = jnp.zeros((5, 128), F32)
    for step in range(count):
        back = count - 1 - step
        out_ref[9 * step : 9 * step + 4] = value[:4]
        left_ref[step : step + 1] = value[4:]
        out_ref[9 * back + 5 : 9 * back + 9] = other[1:]
        right_ref[back : back + 1] = other[:1]
        value = gains[step : step + 1] * value + in_ref[10 * step : 10 * step + 5]
        other = gains[back : back + 1] * other + in_ref[10 * back + 4 : 10 * back + 9]
    out_ref[pl.ds(4, count, stride=9), :] = jnp.where(
        low_lanes(count), left_ref[...], right_ref[...]
    )


def expand_kernel(count, home_ref, came_ref, out_ref):
    value, other = unpack(home_ref, count)
    for part in range(ROW):
        back = ROW - 1 - part
        ahead, _, gain = row_parts(came_ref, part)
        out_ref[part, :QUARTER] = value
        value = gain * value + ahead
        _, behind, gain = row_parts(came_ref, back)
        other = gain * other + behind
        out_ref[back, QUARTER:] = other


def finish_kernel(rows_img, in_ref, st_hbm, out_ref, adj_ref):
    value = jnp.concatenate([in_ref[part, :QUARTER] for part in range(ROW)], axis=0)
    other = jnp.concatenate([in_ref[part, QUARTER:] for part in range(ROW)], axis=0)
    from_tiles(out_ref, value, rows_img)
    from_tiles(adj_ref, other, rows_img)

    @pl.when(lax.axis_index("layer") == 0)
    def _():
        pltpu.sync_copy(st_hbm, out_ref)


def call(kernel, outs, *args, flops=0, anywhere=(), away=(), scratch=(), room=VMEM_BYTES):
    shapes = [jax.ShapeDtypeStruct(s, d) for s, d in outs]
    size = sum(a.size * a.dtype.itemsize for a in list(args) + shapes)
    near = pl.BlockSpec(memory_space=pltpu.VMEM)
    far = pl.BlockSpec(memory_space=pltpu.HBM)
    return pl.pallas_call(
        kernel,
        out_shape=shapes,
        in_specs=[far if i in anywhere else near for i in range(len(args))],
        out_specs=[far if i in away else near for i in range(len(outs))],
        scratch_shapes=list(scratch),
        compiler_params=pltpu.CompilerParams(vmem_limit_bytes=room),
        cost_estimate=pl.CostEstimate(flops=flops, bytes_accessed=size, transcendentals=0),
    )(*args)


def exchange(array, groups):
    count = len(groups[0])
    moved = lax.all_to_all(
        array.reshape(count, -1, 128) if array.ndim == 3 else array.reshape(count, -1),
        "layer",
        0,
        0,
        axis_index_groups=groups,
        tiled=True,
    )
    return moved.reshape(array.shape)


def body(states, adjoints, kernels, biases, coarse_gain):
    rows_img, flat = states.shape[2:]
    depth_count = kernels.shape[0]
    blocks, parts = lax.axis_size("layer"), lax.axis_size("dp")
    tiles = rows_img * flat // 128
    count = blocks // ROW
    rows = [[z * ROW + x for x in range(ROW)] for z in range(count)]
    columns = [[z * ROW + x for z in range(count)] for x in range(ROW)]
    state = states.reshape(rows_img, flat)
    adjoint = adjoints.reshape(rows_img, flat)
    taps = kernels.reshape(depth_count * 9, 64, 64)
    image = ((rows_img, flat), F32)
    half = ((584, 128), F32)
    swap = [(i, i ^ 1) for i in range(parts)]
    send, give, keep = call(
        functools.partial(block_kernel, depth_count, blocks),
        [((ROW, 2 * QUARTER + 8, 128), F32), half, half],
        state, adjoint, taps, biases, coarse_gain,
        flops=3 * depth_count * tiles * 768 * 256,
        anywhere=(0, 1, 2, 3, 4),
        room=BLOCK_VMEM,
        scratch=(
            pltpu.VMEM(image[0], F32),
            pltpu.VMEM(image[0], F32),
            pltpu.VMEM(taps.shape, BF),
            pltpu.VMEM(biases.shape, F32),
            pltpu.VMEM(coarse_gain.shape, F32),
            pltpu.VMEM((depth_count, tiles, 128), F32),
            pltpu.VMEM((depth_count, tiles, 768), BF),
            pltpu.VMEM((depth_count, tiles, 128), BF),
            pltpu.SemaphoreType.DMA((5,)),
        ),
    )
    came = exchange(send, rows)
    got = lax.ppermute(give, "dp", swap)
    (mine,) = call(functools.partial(add_kernel, 1.0), [half], keep, got)
    (totals,) = call(functools.partial(compose_kernel, count), [((10 * count, 128), F32)], came)
    column = exchange(totals, columns)
    got = lax.ppermute(mine, "dp", [(i, i ^ 2) for i in range(parts)])
    (before,) = call(
        functools.partial(scan_kernel, count),
        [((9 * count, 128), F32)],
        column,
        scratch=(pltpu.VMEM((count, 128), F32), pltpu.VMEM((count, 128), F32)),
    )
    home = exchange(before, columns)
    (mine,) = call(functools.partial(add_kernel, 1.0), [half], mine, got)
    got = lax.ppermute(mine, "dp", [(i, i ^ 4) for i in range(parts)])
    (mine,) = call(functools.partial(add_kernel, 1.0 / parts), [half], mine, got)
    theirs = lax.ppermute(mine, "dp", swap)
    (spread,) = call(
        functools.partial(expand_kernel, count),
        [((ROW, 2 * QUARTER, 128), F32)],
        home, came,
    )
    result = exchange(spread, rows)
    grad, bias_grad = call(
        functools.partial(spread_kernel, depth_count),
        [((depth_count * 9, 64, 64), F32), ((depth_count, 64), F32)],
        mine, theirs,
    )
    states_new, adjoints_new = call(
        functools.partial(finish_kernel, rows_img), [image, image], result, state,
        anywhere=(1,),
    )
    return (
        states_new.reshape(states.shape),
        adjoints_new.reshape(adjoints.shape),
        grad.reshape(kernels.shape),
        bias_grad,
    )


def solution(mesh):
    return jax.shard_map(
        body,
        mesh=mesh,
        in_specs=(
            P("layer", "dp", None, None),
            P("layer", "dp", None, None),
            P("layer", None, None, None, None),
            P("layer", None),
            P("layer", None),
        ),
        out_specs=(
            P("layer", "dp", None, None),
            P("layer", "dp", None, None),
            P("layer", None, None, None, None),
            P("layer", None),
        ),
        check_vma=False,
    )
```

```python
import functools

import jax
import jax.numpy as jnp
from jax import lax
from jax.experimental import pallas as pl
from jax.experimental.pallas import tpu as pltpu
from jax.sharding import PartitionSpec as P

STEP = 0.5
BF = jnp.bfloat16
F32 = jnp.float32
VMEM_BYTES = 12 * 1024 * 1024
BLOCK_VMEM = 67_000_000
ROW = 4
LEAD = 11
QUARTER = 72


def low_lanes(rows):
    return lax.broadcasted_iota(jnp.int32, (rows, 128), 1) < 64


def to_tiles(x):
    return jnp.concatenate([x[:, 128 * k : 128 * k + 128] for k in range(x.shape[1] // 128)], axis=0)


def patches(out_ref, v, rows_img):
    count = v.shape[0]
    turned = pltpu.roll(v, 64, 1)
    edge = jnp.zeros((rows_img, 128), F32)
    mid = jnp.where(
        low_lanes(count + rows_img),
        jnp.concatenate([edge, turned], axis=0),
        jnp.concatenate([turned, edge], axis=0),
    )
    tiles = (count + rows_img) // 8
    per = rows_img // 8
    row = lax.broadcasted_iota(jnp.int32, (tiles, 8, 128), 1)
    zero = jnp.zeros((1, 8, 128), F32)
    whole = mid.reshape(tiles, 8, 128)
    turn = pltpu.roll(whole, 1, 1)
    before = jnp.concatenate([zero if i % per == 0 else turn[i - 1 : i] for i in range(tiles)], axis=0)
    up = jnp.where(row == 0, before, turn).reshape(tiles * 8, 128)
    turn = pltpu.roll(whole, 7, 1)
    after = jnp.concatenate(
        [zero if i % per == per - 1 else turn[i + 1 : i + 2] for i in range(tiles)], axis=0
    )
    down = jnp.where(row == 7, after, turn).reshape(tiles * 8, 128)
    for dy, t in enumerate((up, mid, down)):
        out_ref[:, 256 * dy : 256 * dy + 128] = t[:count].astype(BF)
        out_ref[:, 256 * dy + 128 : 256 * dy + 256] = t[rows_img:].astype(BF)


def forward_weights(k_ref, layer):
    zero = jnp.zeros((64, 64), BF)
    rows = []
    for dy in range(3):
        tap = [k_ref[layer * 9 + dy * 3 + dx] for dx in range(3)]
        rows.append(jnp.concatenate([tap[0], zero], axis=1))
        rows.append(jnp.concatenate([tap[1], tap[0]], axis=1))
        rows.append(jnp.concatenate([tap[2], tap[1]], axis=1))
        rows.append(jnp.concatenate([zero, tap[2]], axis=1))
    return jnp.concatenate(rows, axis=0)


def backward_weights(k_ref, layer):
    zero = jnp.zeros((64, 64), BF)
    first, second = [], []
    for dy in range(3):
        tap = [k_ref[layer * 9 + (2 - dy) * 3 + dx] for dx in range(3)]
        first += [tap[2], tap[1], tap[0], zero]
        second += [zero, tap[2], tap[1], tap[0]]
    return jnp.concatenate(
        [jnp.concatenate(first, axis=1), jnp.concatenate(second, axis=1)], axis=0
    )


def pack(out_ref, count, value, other, gain):
    for r in range(4):
        out_ref[pl.ds(r, count, stride=10), :] = value[count * r : count * r + count]
        out_ref[pl.ds(5 + r, count, stride=10), :] = other[count * r : count * r + count]
    low = low_lanes(count // 2)
    rest, rest_other = value[4 * count :], other[4 * count :]
    out_ref[pl.ds(4, count, stride=10), :] = jnp.concatenate(
        [
            jnp.where(low, rest, pltpu.roll(rest_other, 64, 1)),
            jnp.where(low, pltpu.roll(rest, 64, 1), rest_other),
        ],
        axis=0,
    )
    out_ref[pl.ds(9, count, stride=10), :] = jnp.broadcast_to(gain, (count, 128))


def unpack(ref, count):
    low = low_lanes(count // 2)
    extra = ref[pl.ds(4, count, stride=9), :]
    top, bottom = extra[: count // 2], extra[count // 2 :]
    rest = jnp.where(low, top, pltpu.roll(bottom, 64, 1))
    rest_other = jnp.where(low, pltpu.roll(top, 64, 1), bottom)
    value = [ref[pl.ds(r, count, stride=9), :] for r in range(4)]
    other = [ref[pl.ds(5 + r, count, stride=9), :] for r in range(4)]
    return jnp.concatenate(value + [rest], axis=0), jnp.concatenate(other + [rest_other], axis=0)


def from_tiles(out_ref, value, rows_img):
    for k in range(value.shape[0] // rows_img):
        out_ref[:, 128 * k : 128 * k + 128] = value[rows_img * k : rows_img * k + rows_img]


def doubled(row):
    return jnp.concatenate([row, row], axis=1)


def layer_gradient(out_ref, pair, second, cells, sens):
    grad = lax.dot_general(cells, sens, (((0,), (0,)), ((), ())), preferred_element_type=F32)
    low = low_lanes(192)
    for dy in range(3):
        part = grad[256 * dy : 256 * dy + 256]
        rows = slice(192 * dy, 192 * dy + 192)
        if second:
            out_ref[pair, rows] = pltpu.roll(part[:192], 64, 1) + part[64:]
        else:
            tile = part[:192] + pltpu.roll(part[64:], 64, 1)
            out_ref[pair, rows] = jnp.where(low, tile, out_ref[pair, rows])


def block_kernel(
    depth_count,
    blocks,
    st_hbm,
    adj_hbm,
    k_hbm,
    b_hbm,
    g_hbm,
    send_hbm,
    give_hbm,
    keep_hbm,
    st_ref,
    adj_ref,
    k_ref,
    b_ref,
    g_ref,
    act_ref,
    patch_ref,
    send_ref,
    half_ref,
    work_ref,
    in_sems,
    out_sems,
):
    pairs = [(k_hbm, k_ref), (st_hbm, st_ref), (b_hbm, b_ref), (adj_hbm, adj_ref), (g_hbm, g_ref)]
    copies = [pltpu.make_async_copy(a, b, in_sems.at[i]) for i, (a, b) in enumerate(pairs)]
    for copy in copies:
        copy.start()
    rows_img = st_ref.shape[0]
    place = lax.axis_index("layer")
    core = lax.rem(lax.axis_index("dp"), 2)
    for copy in copies[:3]:
        copy.wait()
    start = to_tiles(st_ref[...])
    field = start
    bias = doubled(b_ref[...])
    for layer in range(depth_count):
        patches(patch_ref.at[layer], field, rows_img)
        total = jnp.dot(
            patch_ref[layer], forward_weights(k_ref, layer), preferred_element_type=F32
        )
        act = jnp.tanh(total + bias[layer : layer + 1])
        act_ref[layer] = act
        field = field + STEP * act
    for copy in copies[3:]:
        copy.wait()
    gain = doubled(g_ref[...])
    lead = jnp.where(place == 0, jnp.zeros_like(gain), gain)
    tail = jnp.where(place == blocks - 1, jnp.zeros_like(gain), gain)

    def post(value, at):
        for part in range(ROW):
            send_ref[part, at : at + QUARTER] = value[QUARTER * part : QUARTER * part + QUARTER]

    post(field - lead * start, 0)
    for part in range(ROW):
        send_ref[part, 2 * QUARTER :] = jnp.broadcast_to(gain, (8, 128))
    ahead = pl.ds(0, QUARTER)
    outs = [pltpu.make_async_copy(send_ref.at[:, ahead], send_hbm.at[:, ahead], out_sems.at[0])]
    outs[-1].start()
    start_adj = to_tiles(adj_ref[...])
    adjoint = start_adj
    sums = [None] * depth_count
    for layer in reversed(range(depth_count)):
        act = act_ref[layer]
        sens = STEP * (1.0 - act * act) * adjoint
        total = jnp.sum(sens, axis=0, keepdims=True)
        sums[layer] = total + pltpu.roll(total, 64, 1)
        layer_gradient(half_ref, layer // 2, layer % 2 == 1, patch_ref[layer], sens.astype(BF))
        if layer == 0:
            for pair in range(2):
                half_ref[pair, 576:584] = jnp.concatenate(
                    sums + [jnp.zeros((8 - depth_count, 128), F32)], axis=0
                )
            for i, (pair, ref) in enumerate(((1 - core, give_hbm), (core, keep_hbm))):
                outs.append(pltpu.make_async_copy(half_ref.at[pair], ref, out_sems.at[1 + i]))
                outs[-1].start()
        patches(work_ref.at[layer], sens, rows_img)
        adjoint = adjoint + lax.dot_general(
            work_ref[layer],
            backward_weights(k_ref, layer),
            (((1,), (1,)), ((), ())),
            preferred_element_type=F32,
        )
    post(adjoint - tail * start_adj, QUARTER)
    behind = pl.ds(QUARTER, QUARTER + 8)
    outs.append(pltpu.make_async_copy(send_ref.at[:, behind], send_hbm.at[:, behind], out_sems.at[3]))
    outs[-1].start()
    for copy in outs:
        copy.wait()


def add_kernel(scale, own_ref, other_ref, out_ref):
    out_ref[...] = (own_ref[...] + other_ref[...]) * scale


def spread_kernel(depth_count, own_ref, other_ref, grad_ref, bias_ref):
    core = lax.rem(lax.axis_index("dp"), 2)
    bias_ref[...] = own_ref[576 : 576 + depth_count, :64]
    for pair, ref in ((core, own_ref), (1 - core, other_ref)):
        for tap in range(9):
            tile = ref[64 * tap : 64 * tap + 64]
            grad_ref[18 * pair + tap] = tile[:, :64]
            grad_ref[18 * pair + 9 + tap] = pltpu.roll(tile, 64, 1)[:, :64]


def row_parts(ref, part):
    return (
        ref[part, :QUARTER],
        ref[part, QUARTER : 2 * QUARTER],
        ref[part, 2 * QUARTER : 2 * QUARTER + 1],
    )


def compose_kernel(count, in_ref, out_ref):
    parts = [row_parts(in_ref, part) for part in range(ROW)]
    value, other, gain = parts[0][0], parts[-1][1], parts[0][2]
    for ahead, _, factor in parts[1:]:
        value = factor * value + ahead
        gain = gain * factor
    for _, behind, factor in reversed(parts[:-1]):
        other = factor * other + behind
    pack(out_ref, count, value, other, gain)


def scan_kernel(count, in_ref, out_ref, left_ref, right_ref):
    gains = in_ref[pl.ds(9, count, stride=10), :]
    value = jnp.zeros((5, 128), F32)
    other = jnp.zeros((5, 128), F32)
    for step in range(count):
        at = (step - LEAD) % count
        back = (count - 1 - step - LEAD) % count
        out_ref[9 * at : 9 * at + 4] = value[:4]
        left_ref[at : at + 1] = value[4:]
        out_ref[9 * back + 5 : 9 * back + 9] = other[1:]
        right_ref[back : back + 1] = other[:1]
        value = gains[at : at + 1] * value + in_ref[10 * at : 10 * at + 5]
        other = gains[back : back + 1] * other + in_ref[10 * back + 4 : 10 * back + 9]
    out_ref[pl.ds(4, count, stride=9), :] = jnp.where(
        low_lanes(count), left_ref[...], right_ref[...]
    )


def expand_kernel(count, home_ref, came_ref, out_ref):
    value, other = unpack(home_ref, count)
    for part in range(ROW):
        back = ROW - 1 - part
        ahead, _, gain = row_parts(came_ref, part)
        out_ref[part, :QUARTER] = value
        value = gain * value + ahead
        _, behind, gain = row_parts(came_ref, back)
        other = gain * other + behind
        out_ref[back, QUARTER:] = other


def finish_kernel(rows_img, in_ref, st_ref, out_ref, adj_ref):
    other = jnp.concatenate([in_ref[part, QUARTER:] for part in range(ROW)], axis=0)
    from_tiles(adj_ref, other, rows_img)

    @pl.when(lax.axis_index("layer") > 0)
    def _():
        value = jnp.concatenate([in_ref[part, :QUARTER] for part in range(ROW)], axis=0)
        from_tiles(out_ref, value, rows_img)

    @pl.when(lax.axis_index("layer") == 0)
    def _():
        out_ref[...] = st_ref[...]


def call(kernel, outs, *args, flops=0, anywhere=(), away=(), scratch=(), room=VMEM_BYTES):
    shapes = [jax.ShapeDtypeStruct(s, d) for s, d in outs]
    size = sum(a.size * a.dtype.itemsize for a in list(args) + shapes)
    near = pl.BlockSpec(memory_space=pltpu.VMEM)
    far = pl.BlockSpec(memory_space=pltpu.HBM)
    return pl.pallas_call(
        kernel,
        out_shape=shapes,
        in_specs=[far if i in anywhere else near for i in range(len(args))],
        out_specs=[far if i in away else near for i in range(len(outs))],
        scratch_shapes=list(scratch),
        compiler_params=pltpu.CompilerParams(vmem_limit_bytes=room),
        cost_estimate=pl.CostEstimate(flops=flops, bytes_accessed=size, transcendentals=0),
    )(*args)


def exchange(array, groups):
    count = len(groups[0])
    moved = lax.all_to_all(
        array.reshape(count, -1, 128) if array.ndim == 3 else array.reshape(count, -1),
        "layer",
        0,
        0,
        axis_index_groups=groups,
        tiled=True,
    )
    return moved.reshape(array.shape)


def body(states, adjoints, kernels, biases, coarse_gain):
    rows_img, flat = states.shape[2:]
    depth_count = kernels.shape[0]
    blocks, parts = lax.axis_size("layer"), lax.axis_size("dp")
    tiles = rows_img * flat // 128
    count = blocks // ROW
    rows = [[z * ROW + x for x in range(ROW)] for z in range(count)]
    columns = [[(z + LEAD) % count * ROW + x for z in range(count)] for x in range(ROW)]
    state = states.reshape(rows_img, flat)
    adjoint = adjoints.reshape(rows_img, flat)
    taps = kernels.reshape(depth_count * 9, 64, 64)
    image = ((rows_img, flat), F32)
    half = ((584, 128), F32)
    swap = [(i, i ^ 1) for i in range(parts)]
    send, give, keep = call(
        functools.partial(block_kernel, depth_count, blocks),
        [((ROW, 2 * QUARTER + 8, 128), F32), half, half],
        state, adjoint, taps, biases, coarse_gain,
        flops=3 * depth_count * tiles * 768 * 256,
        anywhere=(0, 1, 2, 3, 4),
        away=(0, 1, 2),
        room=BLOCK_VMEM,
        scratch=(
            pltpu.VMEM(image[0], F32),
            pltpu.VMEM(image[0], F32),
            pltpu.VMEM(taps.shape, BF),
            pltpu.VMEM(biases.shape, F32),
            pltpu.VMEM(coarse_gain.shape, F32),
            pltpu.VMEM((depth_count, tiles, 128), F32),
            pltpu.VMEM((depth_count, tiles, 768), BF),
            pltpu.VMEM((ROW, 2 * QUARTER + 8, 128), F32),
            pltpu.VMEM((2,) + half[0], F32),
            pltpu.VMEM((depth_count, tiles, 768), BF),
            pltpu.SemaphoreType.DMA((5,)),
            pltpu.SemaphoreType.DMA((4,)),
        ),
    )
    came = exchange(send, rows)
    got = lax.ppermute(give, "dp", swap)
    (mine,) = call(functools.partial(add_kernel, 1.0), [half], keep, got)
    (totals,) = call(functools.partial(compose_kernel, count), [((10 * count, 128), F32)], came)
    column = exchange(totals, columns)
    got = lax.ppermute(mine, "dp", [(i, i ^ 2) for i in range(parts)])
    (before,) = call(
        functools.partial(scan_kernel, count),
        [((9 * count, 128), F32)],
        column,
        scratch=(pltpu.VMEM((count, 128), F32), pltpu.VMEM((count, 128), F32)),
    )
    home = exchange(before, columns)
    (mine,) = call(functools.partial(add_kernel, 1.0), [half], mine, got)
    got = lax.ppermute(mine, "dp", [(i, i ^ 4) for i in range(parts)])
    (mine,) = call(functools.partial(add_kernel, 1.0 / parts), [half], mine, got)
    theirs = lax.ppermute(mine, "dp", swap)
    (spread,) = call(
        functools.partial(expand_kernel, count),
        [((ROW, 2 * QUARTER, 128), F32)],
        home, came,
    )
    result = exchange(spread, rows)
    grad, bias_grad = call(
        functools.partial(spread_kernel, depth_count),
        [((depth_count * 9, 64, 64), F32), ((depth_count, 64), F32)],
        mine, theirs,
    )
    states_new, adjoints_new = call(
        functools.partial(finish_kernel, rows_img), [image, image], result, state
    )
    return (
        states_new.reshape(states.shape),
        adjoints_new.reshape(adjoints.shape),
        grad.reshape(kernels.shape),
        bias_grad,
    )


def solution(mesh):
    return jax.shard_map(
        body,
        mesh=mesh,
        in_specs=(
            P("layer", "dp", None, None),
            P("layer", "dp", None, None),
            P("layer", None, None, None, None),
            P("layer", None),
            P("layer", None),
        ),
        out_specs=(
            P("layer", "dp", None, None),
            P("layer", "dp", None, None),
            P("layer", None, None, None, None),
            P("layer", None),
        ),
        check_vma=False,
    )
```
